256 devices in a mesh: segment: 4 (over y), seq: 64 (over x, z, core).
Axes of the slice: x: 4, y: 4, z: 8, core: 2. Of those that a mesh axis runs over, the one named last changes fastest.
Arguments:
- held: bfloat16 [4, 8192, 1024], P('segment', 'seq'), may hold values from -6 to 6
- log_decay: float32 [4, 8192, 8], P('segment', 'seq'), may hold values from -2 to 0, as said below
- route_ids: int32 [4, 64, 1], P('segment'), may hold values from 0 to 7; in each aligned block of 8 rows (0 to 7, 8 to 15, ..., all dimensions but the last counted through in order) at most 2 rows name the same one
- norm_gain: float32 [4, 1024], P('segment'), may hold values from 0.1 to 1.9
- qkv_weight: bfloat16 [4, 1024, 3072], P('segment'), may hold values from -0.1875 to 0.1875
- beta_weight: bfloat16 [4, 1024, 8], P('segment'), may hold values from -0.1875 to 0.1875
- out_gain: float32 [4, 128], P('segment'), may hold values from 0.1 to 1.9
- out_weight: bfloat16 [4, 1024, 1024], P('segment'), may hold values from -0.1875 to 0.1875
- ffn_gain: float32 [4, 1024], P('segment'), may hold values from 0.1 to 1.9
- gate_weight: bfloat16 [4, 64, 1024, 512], P('segment', 'seq'), may hold values from -0.1875 to 0.1875
- up_weight: bfloat16 [4, 64, 1024, 512], P('segment', 'seq'), may hold values from -0.1875 to 0.1875
- down_weight: bfloat16 [4, 64, 512, 1024], P('segment', 'seq'), may hold values from -0.09375 to 0.09375
Outputs:
- next_held: bfloat16 [4, 8192, 1024], P('segment', 'seq')
The draws below stay inside these ranges and needn't reach their ends.
Inputs may be any that keep to these rules, and one draw needn't show every extreme that they name: `log_decay`: every entry is negative. `route_ids`: within each aligned group of 8 consecutive blocks of a section no machine type is named more than 2 times, and in some group of every draw one type is named exactly 2 times.
All inputs are finite; a program needn't handle non-finite values.
Results may differ from the reference program's by a relative error of at most 0.018.
Values may be sent and summed in bfloat16 or wider, within the bound.
A program may use at most 192 MiB of HBM per device.

```python
import math
from functools import partial
import jax
import jax.numpy as jnp
import numpy as np
from jax import lax

D = 1024
ATTENTION_GROUPS = 8
HEAD = 128
FF = 4096
EXPERTS = 8
BLOCK = 128
TOK_DEV = 128
RELAY_LEGS = 4
MOMENT_TOTAL = 8192
NBLOCKS = 64
SLICES = 8
FF_SLICE = 512
SHARDS = 64
GROUP_BLOCKS = 8
CAP = 2


def draw_log_decay(key, part):
    lookup_vectors = jax.random.split(key, 8)
    fast_share = 0.5
    rough = jax.random.uniform(lookup_vectors[0], (RELAY_LEGS, MOMENT_TOTAL, ATTENTION_GROUPS), jnp.float32, 0.5, 1.5)
    fast = jax.random.uniform(lookup_vectors[1], (RELAY_LEGS, 1, ATTENTION_GROUPS), jnp.float32) < fast_share
    fast_rate = jnp.exp(jax.random.uniform(lookup_vectors[2], (RELAY_LEGS, 1, ATTENTION_GROUPS), jnp.float32, jnp.log(2.0), jnp.log(4.0))) / BLOCK
    slow_rate = jnp.exp(jax.random.uniform(lookup_vectors[3], (RELAY_LEGS, 1, ATTENTION_GROUPS), jnp.float32, jnp.log(0.1), jnp.log(0.25))) / MOMENT_TOTAL
    rate = jnp.where(fast, fast_rate, slow_rate)
    device_factor = jnp.exp(jax.random.uniform(lookup_vectors[4], (RELAY_LEGS, MOMENT_TOTAL // TOK_DEV, 1, ATTENTION_GROUPS), jnp.float32, jnp.log(0.5), jnp.log(2.0)))
    device_factor = jnp.broadcast_to(device_factor, (RELAY_LEGS, MOMENT_TOTAL // TOK_DEV, TOK_DEV, ATTENTION_GROUPS)).reshape(RELAY_LEGS, MOMENT_TOTAL, ATTENTION_GROUPS)
    anchor_index = -rate * rough * device_factor
    leading_packet = jax.random.randint(lookup_vectors[5], (RELAY_LEGS, 1, 1, ATTENTION_GROUPS), 0, MOMENT_TOTAL)
    initial_shift = jax.random.randint(lookup_vectors[7], (RELAY_LEGS, 1, 1, ATTENTION_GROUPS), 1, MOMENT_TOTAL)
    trailing_packet = (leading_packet + initial_shift) % MOMENT_TOTAL
    packet_locus = jnp.concatenate([leading_packet, trailing_packet], axis=2)
    stratum_level = jnp.log(jax.random.uniform(lookup_vectors[6], (RELAY_LEGS, 1, 2, ATTENTION_GROUPS), jnp.float32, 0.55, 0.8))
    moment_number = jnp.arange(MOMENT_TOTAL).reshape(1, MOMENT_TOTAL, 1, 1)
    symbol_packet = jnp.sum(jnp.where(moment_number == packet_locus, stratum_level, 0.0), axis=2)
    return (anchor_index + symbol_packet).astype(jnp.float32)


def shard_levels(stream_key, dims, cuts, smallest, top_value):
    factor_of = 1.0
    for dim, shards_of in cuts:
        steps = jax.random.uniform(jax.random.fold_in(jax.random.fold_in(stream_key, 6), dim), (shards_of,), jnp.float32, smallest / len(cuts), top_value / len(cuts))
        factor_of = factor_of * jnp.repeat(jnp.exp(steps), dims[dim] // shards_of).reshape((-1,) + (1,) * (len(dims) - 1 - dim))
    return factor_of


def routed_block(own_key, own, number, rows, amount, top, most, lean):
    sequence = jax.random.permutation(own_key, amount)
    heavy_load, usual = shares(amount, rows * top, most, lean, True), shares(amount, rows * top, most, lean, False)
    places = jnp.arange(amount)

    def named(lengths, offset_by):
        used = int((lengths > 0).sum())
        fixed = max(1, used // 4)
        shifted = fixed + (places - fixed + offset_by * (used - fixed)) % max(1, amount - fixed)
        return jnp.zeros((amount,), jnp.int32).at[sequence[jnp.where(places < fixed, places, shifted)]].set(jnp.asarray(lengths, jnp.int32))

    lengths = jnp.where(number % 4 == 0, named(heavy_load, number // 4), named(usual, number - number // 4 - 1))
    mixed = jax.random.permutation(jax.random.fold_in(own, 3), amount)
    donor, sink = mixed[0:amount // 2 * 2:2], mixed[1:amount // 2 * 2:2]
    slack = jnp.minimum(lengths[donor] - 1, most - lengths[sink]) // 2
    slack = jnp.where((donor == sequence[0]) | (sink == sequence[0]) | (lengths[sink] == 0), 0, jnp.maximum(slack, 0))
    shifted = jax.random.randint(jax.random.fold_in(own, 4), (amount // 2,), 0, 1 << 20) % (slack + 1)
    lengths = lengths.at[donor].add(-shifted).at[sink].add(shifted)
    members = jnp.searchsorted(jnp.cumsum(lengths), jnp.arange(rows * top), side="right").astype(jnp.int32)
    table = members.reshape(top, rows).T
    table = table[jax.random.permutation(jax.random.fold_in(own, 1), rows)]
    offset_by = jax.random.randint(jax.random.fold_in(own, 2), (rows, 1), 0, top)
    return jnp.take_along_axis(table, (jnp.arange(top)[None, :] + offset_by) % top, axis=1)


def shares(number_of, total, reach, lean, full):
    portions = [(1 << 20) // math.isqrt(standing ** lean) + 1 for standing in range(1, number_of + 1)]
    largest = reach if full else min(reach, max(-(-total // number_of), total * portions[0] // sum(portions)))
    least = 1 if total - largest >= number_of - 1 else 0
    holding, rest = [largest] + [least] * (number_of - 1), total - largest - least * (number_of - 1)
    while rest > 0:
        candidates = [i for i in range(1, number_of) if holding[i] < largest] or [i for i in range(1, number_of) if holding[i] < reach]
        mass, remaining = sum([portions[i] for i in candidates]), rest
        for i in candidates:
            extra = min(reach - holding[i], max(1, remaining * portions[i] // mass), rest)
            holding[i] = holding[i] + extra
            rest = rest - extra
    return np.array(holding)


def gaussian(stream_key, dims, width, most, cuts=(), held_as=jnp.bfloat16):
    array = jax.random.normal(stream_key, dims, jnp.float32) * width
    if len(cuts) > 0:
        array = shard_levels(stream_key, dims, cuts, -0.22, 0.18) * array
    return jnp.clip(array, min=-most, max=most).astype(held_as)


def setup_inputs(seed: int = 0) -> dict:
    seeds = jax.random.split(jax.random.key(seed), 13)
    held = gaussian(seeds[0], (RELAY_LEGS, MOMENT_TOTAL, D), 1.0, 6.0, ((0, 4), (1, 64)))
    log_decay = draw_log_decay(jax.random.fold_in(seeds[12], 71), 0)
    route_ids_keys = jax.random.split(jax.random.fold_in(seeds[2], 1), RELAY_LEGS * NBLOCKS // GROUP_BLOCKS)
    route_ids_turns = jax.random.permutation(jax.random.fold_in(seeds[2], 3), RELAY_LEGS * NBLOCKS // GROUP_BLOCKS)
    route_ids = jax.vmap(lambda own, number: routed_block(jax.random.fold_in(seeds[2], 2), own, number, GROUP_BLOCKS, EXPERTS, 1, CAP, 2))(route_ids_keys, route_ids_turns).reshape((RELAY_LEGS, NBLOCKS, 1))
    norm_gain = jnp.clip(1.0 + 0.18 * jax.random.normal(seeds[3], (RELAY_LEGS, D), jnp.float32), 0.1, 1.9)
    qkv_weight = gaussian(seeds[4], (RELAY_LEGS, D, 3 * D), D ** -0.5, 0.1875, ((0, 4),))
    beta_weight = gaussian(seeds[5], (RELAY_LEGS, D, ATTENTION_GROUPS), D ** -0.5, 0.1875, ((0, 4),))
    out_gain = jnp.clip(1.0 + 0.18 * jax.random.normal(seeds[6], (RELAY_LEGS, HEAD), jnp.float32), 0.1, 1.9)
    out_weight = gaussian(seeds[7], (RELAY_LEGS, D, D), D ** -0.5, 0.1875, ((0, 4),))
    ffn_gain = jnp.clip(1.0 + 0.18 * jax.random.normal(seeds[8], (RELAY_LEGS, D), jnp.float32), 0.1, 1.9)
    gate_weight = gaussian(seeds[9], (RELAY_LEGS, SHARDS, D, FF_SLICE), D ** -0.5, 0.1875, ((0, 4), (1, 64)))
    up_weight = gaussian(seeds[10], (RELAY_LEGS, SHARDS, D, FF_SLICE), D ** -0.5, 0.1875, ((0, 4), (1, 64)))
    down_weight = gaussian(seeds[11], (RELAY_LEGS, SHARDS, FF_SLICE, D), FF ** -0.5, 0.09375, ((0, 4), (1, 64)))
    return dict(held=held, log_decay=log_decay, route_ids=route_ids, norm_gain=norm_gain, qkv_weight=qkv_weight, beta_weight=beta_weight, out_gain=out_gain, out_weight=out_weight, ffn_gain=ffn_gain, gate_weight=gate_weight, up_weight=up_weight, down_weight=down_weight)


def rms(values, gain):
    return values * lax.rsqrt(lax.optimization_barrier(jnp.mean(values * values, axis=-1, keepdims=True)) + 1e-06) * gain

def unit_lower_solve(strict_part, rhs):
    ein = partial(jnp.einsum, precision=lax.Precision.HIGHEST)
    length = strict_part.shape[-1]
    raised = -strict_part
    running = jnp.eye(length, dtype=jnp.float32) + raised
    for _ in range((length - 1).bit_length() - 1):
        raised = ein('hij,hjk->hik', raised, raised)
        running = running + ein('hij,hjk->hik', running, raised)
    return ein('hij,hjk->hik', running, rhs)

def span_terms(lookup_vectors, values, beta, logd):
    ein = partial(jnp.einsum, precision=lax.Precision.HIGHEST)
    length = lookup_vectors.shape[1]
    dim_k = lookup_vectors.shape[2]
    cumul = jnp.cumsum(logd, axis=-1)
    posit = jnp.arange(length)
    strict = posit[:, None] > posit[None, :]
    differ = cumul[:, :, None] - cumul[:, None, :]
    ratio = jnp.where(strict, jnp.exp(jnp.where(strict, differ, 0.0)), 0.0)
    inner = ein('htd,hsd->hts', lookup_vectors, lookup_vectors)
    strict_part = beta[:, :, None] * ratio * inner
    growth = jnp.exp(cumul)
    rhs = jnp.concatenate([(beta * growth)[:, :, None] * lookup_vectors, beta[:, :, None] * values], axis=-1)
    solved = unit_lower_solve(strict_part, rhs)
    w_part = solved[..., :dim_k]
    u_part = solved[..., dim_k:]
    tail = jnp.exp(cumul[:, -1:] - cumul)
    scaled = tail[:, :, None] * lookup_vectors
    trans_a = growth[:, -1][:, None, None] * jnp.eye(dim_k, dtype=jnp.float32) - ein('hck,hcj->hkj', w_part, scaled)
    trans_b = ein('hcv,hck->hvk', u_part, scaled)
    return (cumul, w_part, u_part, trans_a, trans_b)

def span_output(queries, lookup_vectors, cumul, w_part, u_part, state):
    ein = partial(jnp.einsum, precision=lax.Precision.HIGHEST)
    length = lookup_vectors.shape[1]
    posit = jnp.arange(length)
    incl = posit[:, None] >= posit[None, :]
    differ = cumul[:, :, None] - cumul[:, None, :]
    ratio = jnp.where(incl, jnp.exp(jnp.where(incl, differ, 0.0)), 0.0)
    update = u_part - ein('hck,hvk->hcv', w_part, state)
    scores = ein('htd,hsd->hts', queries, lookup_vectors) * ratio
    return jnp.exp(cumul)[:, :, None] * ein('hck,hvk->hcv', queries, state) + ein('hts,hsv->htv', scores, update)

def one_section(x, logd, ids, norm_g, w_qkv, w_beta, out_g, w_out, ffn_g, w_gate, w_up, w_down):
    ein = partial(jnp.einsum, precision=lax.Precision.HIGHEST)
    xf = x.astype(jnp.float32)
    xn = rms(xf, norm_g).astype(jnp.bfloat16)
    qkv = jnp.dot(xn, w_qkv, preferred_element_type=jnp.float32).astype(jnp.bfloat16).astype(jnp.float32)
    queries = qkv[:, :D].reshape(MOMENT_TOTAL, ATTENTION_GROUPS, HEAD)
    lookup_vectors = qkv[:, D:2 * D].reshape(MOMENT_TOTAL, ATTENTION_GROUPS, HEAD)
    values = qkv[:, 2 * D:].reshape(MOMENT_TOTAL, ATTENTION_GROUPS, HEAD)
    queries = queries * lax.rsqrt(lax.optimization_barrier(jnp.sum(queries * queries, axis=-1, keepdims=True)) + 1e-06)
    lookup_vectors = lookup_vectors * lax.rsqrt(lax.optimization_barrier(jnp.sum(lookup_vectors * lookup_vectors, axis=-1, keepdims=True)) + 1e-06)
    beta = jax.nn.sigmoid(jnp.dot(xn, w_beta, preferred_element_type=jnp.float32))
    spans = MOMENT_TOTAL // BLOCK

    def arrange(arr):
        return arr.reshape(spans, BLOCK, ATTENTION_GROUPS, HEAD).transpose(0, 2, 1, 3)
    q_c = arrange(queries)
    k_c = arrange(lookup_vectors)
    v_c = arrange(values)
    b_c = beta.reshape(spans, BLOCK, ATTENTION_GROUPS).transpose(0, 2, 1)
    l_c = logd.reshape(spans, BLOCK, ATTENTION_GROUPS).transpose(0, 2, 1)

    def advance(state, pieces):
        q_one, k_one, v_one, b_one, l_one = pieces
        cumul, w_part, u_part, trans_a, trans_b = span_terms(k_one, v_one, b_one, l_one)
        result = span_output(q_one, k_one, cumul, w_part, u_part, state)
        return (ein('hvk,hkj->hvj', state, trans_a) + trans_b, result)
    start = jnp.zeros((ATTENTION_GROUPS, HEAD, HEAD), jnp.float32)
    final, outs = lax.scan(advance, start, (q_c, k_c, v_c, b_c, l_c))
    mixed = outs.transpose(0, 2, 1, 3).reshape(MOMENT_TOTAL, ATTENTION_GROUPS, HEAD)
    normed = rms(mixed, out_g).astype(jnp.bfloat16).reshape(MOMENT_TOTAL, D)
    hidden = (xf + jnp.dot(normed, w_out, preferred_element_type=jnp.float32)).astype(jnp.bfloat16)
    hn = rms(hidden.astype(jnp.float32), ffn_g).astype(jnp.bfloat16)
    blocks = hn.reshape(NBLOCKS, BLOCK, D)

    def expert_block(args):
        rows, kind = args
        index = (jnp.arange(SLICES) * EXPERTS + kind).astype(jnp.int32)
        gate_all = jnp.take(w_gate, index, axis=0).transpose(1, 0, 2).reshape(D, SLICES * FF_SLICE)
        up_all = jnp.take(w_up, index, axis=0).transpose(1, 0, 2).reshape(D, SLICES * FF_SLICE)
        down_all = jnp.take(w_down, index, axis=0).reshape(SLICES * FF_SLICE, D)
        gate = jnp.dot(rows, gate_all, preferred_element_type=jnp.float32)
        up_val = jnp.dot(rows, up_all, preferred_element_type=jnp.float32)
        act = (jax.nn.silu(gate) * up_val).astype(jnp.bfloat16)
        return jnp.dot(act, down_all, preferred_element_type=jnp.float32).astype(jnp.bfloat16)
    ffn = lax.map(expert_block, (blocks, ids[:, 0])).reshape(MOMENT_TOTAL, D)
    return (hidden.astype(jnp.float32) + ffn.astype(jnp.float32)).astype(jnp.bfloat16)

def reference(held, log_decay, route_ids, norm_gain, qkv_weight, beta_weight, out_gain, out_weight, ffn_gain, gate_weight, up_weight, down_weight):
    outs = []
    for section in range(RELAY_LEGS):
        outs.append(one_section(held[section], log_decay[section], route_ids[section], norm_gain[section], qkv_weight[section], beta_weight[section], out_gain[section], out_weight[section], ffn_gain[section], gate_weight[section], up_weight[section], down_weight[section]))
    stacked = jnp.stack(outs, axis=0)
    return jnp.roll(stacked, 1, axis=0)
```

```python
from functools import partial

import jax
import jax.numpy as jnp
from jax import lax
from jax.experimental import pallas as pl
from jax.experimental.pallas import tpu as pltpu
from jax.sharding import PartitionSpec as P

EXPERTS = 8


def rms(values, gain):
    return values * lax.rsqrt(jnp.mean(values * values, axis=-1, keepdims=True) + 1e-06) * gain


def unit_lower_solve(strict_part, rhs):
    ein = partial(jnp.einsum, precision=lax.Precision.HIGHEST)
    length = strict_part.shape[-1]
    raised = -strict_part
    running = jnp.eye(length, dtype=jnp.float32) + raised
    for _ in range((length - 1).bit_length() - 1):
        raised = ein("hij,hjk->hik", raised, raised)
        running = running + ein("hij,hjk->hik", running, raised)
    return ein("hij,hjk->hik", running, rhs)


def span_terms(lookup_vectors, values, beta, logd):
    ein = partial(jnp.einsum, precision=lax.Precision.HIGHEST)
    length = lookup_vectors.shape[1]
    dim_k = lookup_vectors.shape[2]
    cumul = jnp.cumsum(logd, axis=-1)
    posit = jnp.arange(length)
    strict = posit[:, None] > posit[None, :]
    differ = cumul[:, :, None] - cumul[:, None, :]
    ratio = jnp.where(strict, jnp.exp(jnp.where(strict, differ, 0.0)), 0.0)
    inner = ein("htd,hsd->hts", lookup_vectors, lookup_vectors)
    strict_part = beta[:, :, None] * ratio * inner
    growth = jnp.exp(cumul)
    rhs = jnp.concatenate(
        [(beta * growth)[:, :, None] * lookup_vectors, beta[:, :, None] * values], axis=-1
    )
    solved = unit_lower_solve(strict_part, rhs)
    w_part = solved[..., :dim_k]
    u_part = solved[..., dim_k:]
    tail = jnp.exp(cumul[:, -1:] - cumul)
    scaled = tail[:, :, None] * lookup_vectors
    trans_a = growth[:, -1][:, None, None] * jnp.eye(dim_k, dtype=jnp.float32) - ein(
        "hck,hcj->hkj", w_part, scaled
    )
    trans_b = ein("hcv,hck->hvk", u_part, scaled)
    return (cumul, w_part, u_part, trans_a, trans_b)


LEG = ("segment", "seq")
MESH = pl.DeviceIdType.MESH
NCH = 4
CW = 256
F32 = jnp.float32
BF16 = jnp.bfloat16


def hdot(a, b):
    return jnp.dot(a, b, precision=lax.Precision.HIGHEST, preferred_element_type=F32)


def tick_kernel(
    sel_ref, tgt_ref, ab_ref, qp_ref, o0_ref, x_ref, og_ref, wo_ref, fg_ref,
    gate_hbm, up_hbm, down_hbm,
    out_ref,
    ab_in, tp, tot_out, tot_in, s_out, s_in, on, hid, gath, xs, wg, wu, wd, act, part,
    pout, pin, sr, sl, rr, rl, yout, entering,
    lsem, a2a_s, a2a_r, tot_s, tot_r, st_s, st_r, w_s, w_r, ag_s, ag_r, pf_s, pf_r,
    px_s, px_r, rr_s, rr_r, rl_s, rl_r, y_s, y_r,
):
    seg = lax.axis_index("segment")
    me = lax.axis_index("seq")
    col = me // 16
    z = lax.rem(me // 2, 8)
    core = lax.rem(me, 2)
    grp = me // 8
    i = lax.rem(me, 8)

    def at(xx, zz, cc):
        return (seg, (xx * 8 + zz) * 2 + cc)

    def remote(src, dst, ssem, rsem, dev):
        return pltpu.make_async_remote_copy(
            src_ref=src, dst_ref=dst, send_sem=ssem, recv_sem=rsem,
            device_id=dev, device_id_type=MESH,
        )

    right = at(col, lax.rem(z + 1, 8), core)
    left = at(col, lax.rem(z + 7, 8), core)
    mate = at(col, z, 1 - core)
    xr = at(lax.rem(col + 1, 4), z, core)
    xl = at(lax.rem(col + 3, 4), z, core)
    yn = (lax.rem(seg + 1, 4), me)
    yp = (lax.rem(seg + 3, 4), me)

    barrier = pltpu.get_barrier_semaphore()
    for k in range(1, 8):
        pl.semaphore_signal(barrier, inc=1, device_id=(seg, grp * 8 + lax.rem(i + k, 8)), device_id_type=MESH)
        pl.semaphore_signal(barrier, inc=1, device_id=(seg, lax.rem(grp + k, 8) * 8 + i), device_id_type=MESH)
    for d in (right, left, yn, yp):
        pl.semaphore_signal(barrier, inc=1, device_id=d, device_id_type=MESH)
    pl.semaphore_wait(barrier, 18)

    def a2a_copy(h):
        return remote(ab_ref.at[h], ab_in.at[i], a2a_s.at[h], a2a_r.at[i], (seg, grp * 8 + h))

    def a2a_from(j):
        return remote(ab_ref.at[j], ab_in.at[j], a2a_s.at[j], a2a_r.at[j], (seg, grp * 8 + j))

    @pl.loop(1, 8)
    def _(k):
        a2a_copy(lax.rem(i + k, 8)).start()

    xleft, xright = lax.rem(col + 3, 4), lax.rem(col + 1, 4)
    hbms = (gate_hbm, up_hbm, down_hbm)
    bufs = (wg, wu, wd)

    def piece(buf, k):
        rows = 512 if k // 2 < 2 else 256
        return buf.at[pl.ds((k % 2) * rows, rows)]

    def w_own(k, way):
        a = k // 2
        return remote(
            piece(hbms[a], k), piece(bufs[a].at[col], k), w_s.at[way, k], w_r.at[way, k],
            xr if way == 0 else xl,
        )

    relay_of = ((0, 1, 4), (2, 3, 5))

    def w_relay(r, way):
        k = relay_of[way][r]
        a = k // 2
        origin = xleft if way == 0 else xright
        return remote(
            piece(bufs[a].at[origin], k), piece(bufs[a].at[origin], k),
            w_s.at[way, 6 + r], w_r.at[way, 6 + r], xr if way == 0 else xl,
        )

    def w_got(k, way):
        w_own(k, way).wait_recv()

    w_own(0, 0).start()
    w_own(0, 1).start()
    locals_ = [pltpu.make_async_copy(hbms[a], bufs[a].at[col], lsem.at[a]) for a in range(3)]
    for c in locals_:
        c.start()

    ab_in[i] = ab_ref[i]

    @pl.when(i != 0)
    def _():
        a2a_from(0).wait_recv()

    rows = lax.broadcasted_iota(jnp.int32, (256, 128), 0)
    cols = lax.broadcasted_iota(jnp.int32, (256, 128), 1)
    tp[0] = jnp.where(rows == cols, 1.0, 0.0).astype(F32)
    tp[1] = ab_in[0].astype(F32)

    @pl.loop(1, 8)
    def _(j):
        @pl.when(i != j)
        def _():
            a2a_from(j).wait_recv()

        low = ab_in[j].astype(F32)
        tp[j + 1] = hdot(tp[j], low[:128]) + jnp.where(rows >= 128, low, 0.0)

    tot_out[...] = tp[8].astype(BF16)

    def tot_copy(g):
        return remote(tot_out, tot_in.at[grp], tot_s.at[g], tot_r.at[grp], (seg, g * 8 + i))

    def tot_from(g):
        return remote(tot_out, tot_in.at[g], tot_s.at[g], tot_r.at[g], (seg, g * 8 + i))

    @pl.loop(grp + 1, 8)
    def _(g):
        tot_copy(g).start()

    entering[...] = jnp.zeros((128, 128), F32)

    @pl.loop(0, grp)
    def _(g):
        tot_from(g).wait_recv()
        pair = tot_in[g].astype(F32)
        entering[...] = hdot(entering[...], pair[:128]) + pair[128:]

    def st_copy(j):
        return remote(s_out.at[j], s_in.at[i], st_s.at[j], st_r.at[i], (seg, grp * 8 + j))

    def st_from(j):
        return remote(s_out.at[j], s_in.at[j], st_s.at[j], st_r.at[j], (seg, grp * 8 + j))

    @pl.loop(0, 8)
    def _(j):
        pre = tp[j]
        entered = (hdot(entering[...], pre[:128]) + pre[128:]).astype(BF16)
        s_out[j] = entered

        @pl.when(j == i)
        def _():
            s_in[j] = entered

        @pl.when(j != i)
        def _():
            st_copy(j).start()

    for k in range(1, 6):
        w_own(k, 0).start()
        w_own(k, 1).start()
    w_got(0, 0)
    w_relay(0, 0).start()
    w_got(0, 1)

    @pl.loop(0, 8)
    def _(h):
        @pl.when(h != i)
        def _():
            st_from(h).wait_recv()

        o = o0_ref[h] + lax.dot_general(
            qp_ref[h], s_in[h].astype(F32), (((1,), (1,)), ((), ())),
            precision=lax.Precision.HIGHEST, preferred_element_type=F32,
        )
        o = o * lax.rsqrt(jnp.mean(o * o, axis=-1, keepdims=True) + 1e-06) * og_ref[...]
        on[:, pl.ds(pl.multiple_of(h * 128, 128), 128)] = o.astype(BF16)

    hidden = (
        x_ref[...].astype(F32) + jnp.dot(on[...], wo_ref[...], preferred_element_type=F32)
    ).astype(BF16)
    hid[...] = hidden
    hf = hidden.astype(F32)
    hf = hf * lax.rsqrt(jnp.mean(hf * hf, axis=-1, keepdims=True) + 1e-06) * fg_ref[...]
    gath[me - col * 16] = hf.astype(BF16)

    def half(zz, hv):
        return gath.at[lax.rem(zz, 8) * 2 + core, pl.ds(hv * 64, 64)]

    def ag_send(s, hv, way):
        ref = half(z + 8 - s if way == 0 else z + s, hv)
        k = s * 2 + hv
        return remote(ref, ref, ag_s.at[way, k], ag_r.at[way, k], right if way == 0 else left)

    def ag_recv(s, hv, way):
        ref = half(z + 7 - s if way == 0 else z + 1 + s, hv)
        k = s * 2 + hv
        return remote(ref, ref, ag_s.at[way, k], ag_r.at[way, k], right if way == 0 else left)

    def mate_send(dz, hv):
        ref = half(z + dz, hv)
        k = dz * 2 + hv
        return remote(ref, ref, pf_s.at[k], pf_r.at[k], mate)

    def mate_recv(dz, hv):
        ref = gath.at[lax.rem(z + dz, 8) * 2 + 1 - core, pl.ds(hv * 64, 64)]
        k = dz * 2 + hv
        return remote(ref, ref, pf_s.at[k], pf_r.at[k], mate)

    for hv in range(2):
        for way in range(2):
            ag_send(0, hv, way).start()
    for hv in range(2):
        mate_send(0, hv).start()
    for s in range(1, 4):
        for hv in range(2):
            for way in range(2):
                ag_recv(s - 1, hv, way).wait_recv()
                if s < 3 or hv == way:
                    ag_send(s, hv, way).start()
                mate_send(8 - s if way == 0 else s, hv).start()
    w_got(1, 0)
    w_relay(1, 0).start()
    w_got(1, 1)
    w_got(2, 1)
    w_relay(0, 1).start()
    ag_recv(3, 0, 0).wait_recv()
    mate_send(4, 0).start()
    ag_recv(3, 1, 1).wait_recv()
    mate_send(4, 1).start()
    for dz in range(8):
        for hv in range(2):
            mate_recv(dz, hv).wait_recv()

    for k in range(4):
        xs[pl.ds(k * 128, 128)] = gath[sel_ref[k]]

    def hidden_units(src):
        @pl.loop(0, 2)
        def _(n):
            cut = pl.ds(pl.multiple_of(n * 256, 256), 256)
            gate = jnp.dot(xs[...], wg[src, :, cut], preferred_element_type=F32)
            up = jnp.dot(xs[...], wu[src, :, cut], preferred_element_type=F32)
            act[src, :, cut] = (gate / (1.0 + jnp.exp(-gate)) * up).astype(BF16)

    for c in locals_:
        c.wait()
    hidden_units(col)
    w_got(3, 1)
    w_relay(1, 1).start()
    w_got(2, 0)
    w_got(3, 0)
    hidden_units(xleft)
    hidden_units(xright)
    w_got(4, 0)
    w_relay(2, 0).start()
    w_got(5, 1)
    w_relay(2, 1).start()
    w_got(5, 0)
    w_got(4, 1)
    for way in range(2):
        for r in range(2):
            w_relay(r, way).wait_recv()
    hidden_units(lax.rem(col + 2, 4))
    for way in range(2):
        w_relay(2, way).wait_recv()

    def mate_part(n):
        return remote(pout.at[n], pin.at[n], px_s.at[n], px_r.at[n], mate)

    def own_part(n, zz):
        b = lax.rem(zz, 8)
        return part[n, tgt_ref[b * 2 + core]].astype(F32) + pin[n, b].astype(F32)

    def ring(n, s, way):
        src, dst, ss, rs, dev = (sr, rr, rr_s, rr_r, right) if way == 0 else (sl, rl, rl_s, rl_r, left)
        lo, cnt = (way * 64, 64) if s == 0 else (0, 128)
        cut = pl.ds(lo, cnt)
        return remote(src.at[n, s, cut], dst.at[n, s, cut], ss.at[n, s], rs.at[n, s], dev)

    def first(n):
        mate_part(n).wait_recv()
        far = own_part(n, z + 4).astype(BF16)
        sr[n, 0, pl.ds(0, 64)] = far[:64]
        sl[n, 0, pl.ds(64, 64)] = far[64:]
        ring(n, 0, 0).start()
        ring(n, 0, 1).start()

    @pl.loop(0, NCH)
    def _(n):
        cut = pl.ds(pl.multiple_of(n * CW, CW), CW)
        total = jnp.dot(act[0], wd[0, :, cut], preferred_element_type=F32)
        for src in range(1, 4):
            total = total + jnp.dot(act[src], wd[src, :, cut], preferred_element_type=F32)
        for k in range(4):
            part[n, k] = total[k * 128 : (k + 1) * 128].astype(BF16)
        part[n, 4] = jnp.zeros((128, CW), BF16)
        for zz in range(8):
            pout[n, zz] = part[n, tgt_ref[zz * 2 + 1 - core]]
        mate_part(n).start()

        @pl.when(n >= 1)
        def _():
            first(n - 1)

    first(NCH - 1)

    for s in range(1, 4):
        @pl.loop(0, NCH)
        def _(n):
            for way in range(2):
                ring(n, s - 1, way).wait_recv()
                here = own_part(n, z + 4 - s if way == 0 else z + 4 + s)
                buf, got = (sr, rr) if way == 0 else (sl, rl)
                if s == 1:
                    lo, other = way * 64, 64 - way * 64
                    buf[n, s, pl.ds(lo, 64)] = (
                        here[lo : lo + 64] + got[n, 0, pl.ds(lo, 64)].astype(F32)
                    ).astype(BF16)
                    buf[n, s, pl.ds(other, 64)] = here[other : other + 64].astype(BF16)
                else:
                    buf[n, s] = (here + got[n, s - 1].astype(F32)).astype(BF16)
                ring(n, s, way).start()

    def y_send(n):
        cut = pl.ds(pl.multiple_of(n * CW, CW), CW)
        return remote(yout.at[n], out_ref.at[:, cut], y_s.at[n], y_r.at[n], yn)

    @pl.loop(0, NCH)
    def _(n):
        for way in range(2):
            ring(n, 3, way).wait_recv()
        cut = pl.ds(pl.multiple_of(n * CW, CW), CW)
        ffn = (own_part(n, z) + rr[n, 3].astype(F32) + rl[n, 3].astype(F32)).astype(BF16)
        yout[n] = (hid[:, cut].astype(F32) + ffn.astype(F32)).astype(BF16)
        y_send(n).start()

    @pl.loop(1, 8)
    def _(k):
        j = lax.rem(i + k, 8)
        a2a_copy(j).wait_send()
        st_copy(j).wait_send()

    @pl.loop(grp + 1, 8)
    def _(g):
        tot_copy(g).wait_send()

    for way in range(2):
        for k in range(6):
            w_own(k, way).wait_send()
        for r in range(3):
            w_relay(r, way).wait_send()
        for s in range(4):
            for hv in range(2):
                if s < 3 or hv == way:
                    ag_send(s, hv, way).wait_send()
    for dz in range(8):
        for hv in range(2):
            mate_send(dz, hv).wait_send()

    @pl.loop(0, NCH)
    def _(n):
        mate_part(n).wait_send()
        for s in range(4):
            for way in range(2):
                ring(n, s, way).wait_send()
        y_send(n).wait()


def run_tick(sel, tgt, ab, qp, o0, x, og, wo, fg, gate, up, down):
    vmem = pl.BlockSpec(memory_space=pltpu.VMEM)
    smem = pl.BlockSpec(memory_space=pltpu.SMEM)
    hbm = pl.BlockSpec(memory_space=pl.ANY)
    V = pltpu.VMEM
    D = pltpu.SemaphoreType.DMA
    return pl.pallas_call(
        tick_kernel,
        out_shape=jax.ShapeDtypeStruct((128, 1024), BF16),
        in_specs=[smem, smem] + [vmem] * 7 + [hbm] * 3,
        out_specs=vmem,
        scratch_shapes=[
            V((8, 256, 128), BF16), V((9, 256, 128), F32), V((256, 128), BF16),
            V((8, 256, 128), BF16), V((8, 128, 128), BF16), V((8, 128, 128), BF16),
            V((128, 1024), BF16), V((128, 1024), BF16), V((16, 128, 1024), BF16),
            V((512, 1024), BF16), V((4, 1024, 512), BF16), V((4, 1024, 512), BF16),
            V((4, 512, 1024), BF16), V((4, 512, 512), BF16), V((NCH, 5, 128, CW), BF16),
            V((NCH, 8, 128, CW), BF16), V((NCH, 8, 128, CW), BF16),
            V((NCH, 4, 128, CW), BF16), V((NCH, 4, 128, CW), BF16),
            V((NCH, 4, 128, CW), BF16), V((NCH, 4, 128, CW), BF16), V((NCH, 128, CW), BF16),
            V((128, 128), F32),
            D((3,)), D((8,)), D((8,)), D((8,)), D((8,)), D((8,)), D((8,)),
            D((2, 9)), D((2, 9)), D((2, 8)), D((2, 8)), D((16,)), D((16,)),
            D((NCH,)), D((NCH,)), D((NCH, 4)), D((NCH, 4)), D((NCH, 4)), D((NCH, 4)),
            D((NCH,)), D((NCH,)),
        ],
        compiler_params=pltpu.CompilerParams(
            collective_id=0, has_side_effects=True, vmem_limit_bytes=60 * 1024 * 1024
        ),
        name="tick",
    )(sel, tgt, ab, qp, o0, x, og, wo, fg, gate, up, down)


def per_device(
    held, log_decay, route_ids, norm_gain, qkv_weight, beta_weight, out_gain, out_weight,
    ffn_gain, gate_weight, up_weight, down_weight,
):
    ein = partial(jnp.einsum, precision=lax.Precision.HIGHEST)
    x_rows = held[0]
    steps_dev, width = x_rows.shape
    heads = log_decay.shape[2]
    head_dim = width // heads
    xf = x_rows.astype(F32)
    xn = rms(xf, norm_gain[0]).astype(BF16)
    qkv = jnp.dot(xn, qkv_weight[0], preferred_element_type=F32).astype(BF16).astype(F32)
    qkv = qkv.reshape(steps_dev, 3, heads, head_dim).transpose(1, 2, 0, 3)
    q, k, v = qkv[0], qkv[1], qkv[2]
    q = q * lax.rsqrt(jnp.sum(q * q, axis=-1, keepdims=True) + 1e-06)
    k = k * lax.rsqrt(jnp.sum(k * k, axis=-1, keepdims=True) + 1e-06)
    beta = jax.nn.sigmoid(jnp.dot(xn, beta_weight[0], preferred_element_type=F32)).T
    cumul, w_part, u_part, trans_a, trans_b = span_terms(k, v, beta, log_decay[0].T)
    posit = jnp.arange(steps_dev)
    incl = posit[:, None] >= posit[None, :]
    differ = cumul[:, :, None] - cumul[:, None, :]
    ratio = jnp.where(incl, jnp.exp(jnp.where(incl, differ, 0.0)), 0.0)
    scores = ein("htd,hsd->hts", q, k) * ratio
    qp = jnp.exp(cumul)[:, :, None] * q - ein("hts,hsk->htk", scores, w_part)
    o0 = ein("hts,hsv->htv", scores, u_part)
    ab = jnp.concatenate([trans_a, trans_b], axis=1).astype(BF16)

    place = lax.axis_index("seq")
    kinds = lax.dynamic_slice_in_dim(route_ids[0, :, 0], place // 16 * 16, 16)
    index = jnp.arange(16)
    same = (kinds[:, None] == kinds[None, :]) & (index[:, None] // 8 == index[None, :] // 8)
    rank = jnp.sum((same & (index[None, :] < index[:, None])).astype(jnp.int32), axis=1)
    mine = kinds == place % EXPERTS
    tgt = jnp.where(mine, index // 8 * 2 + rank, 4).astype(jnp.int32)
    slots = jnp.arange(4)
    sel = jnp.sum(jnp.where(tgt[None, :] == slots[:, None], index[None, :], 0), axis=1).astype(
        jnp.int32
    )
    out = run_tick(
        sel, tgt, ab, qp, o0, x_rows, out_gain, out_weight[0], ffn_gain,
        gate_weight[0, 0], up_weight[0, 0], down_weight[0, 0],
    )
    return out[None]


def solution(mesh):
    placed = (
        P("segment", "seq", None),
        P("segment", "seq", None),
        P("segment", None, None),
        P("segment", None),
        P("segment", None, None),
        P("segment", None, None),
        P("segment", None),
        P("segment", None, None),
        P("segment", None),
        P("segment", "seq", None, None),
        P("segment", "seq", None, None),
        P("segment", "seq", None, None),
    )
    return jax.shard_map(
        per_device, mesh=mesh, in_specs=placed, out_specs=P("segment", "seq", None), check_vma=False
    )
```

```python
import jax
import jax.numpy as jnp
from jax import lax
from jax.experimental import pallas as pl
from jax.experimental.pallas import tpu as pltpu
from jax.sharding import PartitionSpec as P

EXPERTS = 8


HU = 4
MESH = pl.DeviceIdType.MESH
NCH = 4
CW = 256
F32 = jnp.float32
BF16 = jnp.bfloat16


def hdot(a, b):
    return jnp.dot(a, b, precision=lax.Precision.HIGHEST, preferred_element_type=F32)


def split_dot(a, b):
    high = a.astype(BF16)
    low = (a - high.astype(F32)).astype(BF16)
    return jnp.dot(high, b, preferred_element_type=F32) + jnp.dot(
        low, b, preferred_element_type=F32
    )


def tick_kernel(
    sel_ref, tgt_ref, x_ref, logd_ref, ng_ref, bw_ref, og_ref, fg_ref,
    wq_hbm, wo_hbm, gate_hbm, up_hbm, down_hbm,
    out_ref,
    wq, wo_ref, qkv, lb, bb, eg, et, qp_ref, o0_ref, ab_ref, ab_in, tp, tot_out, tot_in, s_out, s_in, on, hid, gath, xs, wg, wu, wd, act, part,
    pout, pin, sr, sl, rr, rl, yout, entering,
    lsem, qsem, a2a_s, a2a_r, tot_s, tot_r, st_s, st_r, w_s, w_r, ag_s, ag_r, pf_s, pf_r,
    px_s, px_r, rr_s, rr_r, rl_s, rl_r, y_s, y_r,
):
    seg = lax.axis_index("segment")
    me = lax.axis_index("seq")
    col = me // 16
    z = lax.rem(me // 2, 8)
    core = lax.rem(me, 2)
    grp = me // 8
    i = lax.rem(me, 8)

    def at(xx, zz, cc):
        return (seg, (xx * 8 + zz) * 2 + cc)

    def remote(src, dst, ssem, rsem, dev):
        return pltpu.make_async_remote_copy(
            src_ref=src, dst_ref=dst, send_sem=ssem, recv_sem=rsem,
            device_id=dev, device_id_type=MESH,
        )

    right = at(col, lax.rem(z + 1, 8), core)
    left = at(col, lax.rem(z + 7, 8), core)
    mate = at(col, z, 1 - core)
    xr = at(lax.rem(col + 1, 4), z, core)
    xl = at(lax.rem(col + 3, 4), z, core)
    yn = (lax.rem(seg + 1, 4), me)
    yp = (lax.rem(seg + 3, 4), me)

    fetches = [
        pltpu.make_async_copy(
            wq_hbm.at[:, pl.ds(n * 512, 512)], wq.at[:, pl.ds(n * 512, 512)], qsem.at[n]
        )
        for n in range(6)
    ] + [pltpu.make_async_copy(wo_hbm, wo_ref, qsem.at[6])]
    for c in fetches:
        c.start()

    barrier = pltpu.get_barrier_semaphore()
    for k in range(1, 8):
        pl.semaphore_signal(barrier, inc=1, device_id=(seg, grp * 8 + lax.rem(i + k, 8)), device_id_type=MESH)
        pl.semaphore_signal(barrier, inc=1, device_id=(seg, lax.rem(grp + k, 8) * 8 + i), device_id_type=MESH)
    for d in (right, left, yn, yp):
        pl.semaphore_signal(barrier, inc=1, device_id=d, device_id_type=MESH)
    pl.semaphore_wait(barrier, 18)

    def a2a_copy(h):
        return remote(ab_ref.at[h], ab_in.at[i], a2a_s.at[h], a2a_r.at[i], (seg, grp * 8 + h))

    def a2a_from(j):
        return remote(ab_ref.at[j], ab_in.at[j], a2a_s.at[j], a2a_r.at[j], (seg, grp * 8 + j))

    xleft, xright = lax.rem(col + 3, 4), lax.rem(col + 1, 4)
    hbms = (gate_hbm, up_hbm, down_hbm)
    bufs = (wg, wu, wd)

    def piece(buf, k):
        rows = 512 if k // 2 < 2 else 256
        return buf.at[pl.ds((k % 2) * rows, rows)]

    def w_own(k, way):
        a = k // 2
        return remote(
            piece(hbms[a], k), piece(bufs[a].at[col], k), w_s.at[way, k], w_r.at[way, k],
            xr if way == 0 else xl,
        )

    relay_of = ((0, 1, 4), (2, 3, 5))

    def w_relay(r, way):
        k = relay_of[way][r]
        a = k // 2
        origin = xleft if way == 0 else xright
        return remote(
            piece(bufs[a].at[origin], k), piece(bufs[a].at[origin], k),
            w_s.at[way, 6 + r], w_r.at[way, 6 + r], xr if way == 0 else xl,
        )

    def w_got(k, way):
        w_own(k, way).wait_recv()

    for k in range(3):
        w_own(k, 0).start()
        w_own(k, 1).start()
    locals_ = [pltpu.make_async_copy(hbms[a], bufs[a].at[col], lsem.at[a]) for a in range(3)]
    for c in locals_:
        c.start()

    xf = x_ref[...].astype(F32)
    xn = (
        xf * lax.rsqrt(jnp.mean(xf * xf, axis=-1, keepdims=True) + 1e-06) * ng_ref[...]
    ).astype(BF16)
    for n in range(6):
        fetches[n].wait()
        cut = pl.ds(n * 512, 512)
        qkv[:, cut] = jnp.dot(xn, wq[:, cut], preferred_element_type=F32).astype(BF16)
    beta = jnp.dot(xn, bw_ref[...], preferred_element_type=F32)
    beta = 1.0 / (1.0 + jnp.exp(-beta))
    r128 = lax.broadcasted_iota(jnp.int32, (128, 128), 0)
    c128 = lax.broadcasted_iota(jnp.int32, (128, 128), 1)
    incl = jnp.where(r128 >= c128, 1.0, 0.0).astype(F32)
    upper = jnp.where(r128 < c128, 1.0, 0.0).astype(F32)
    eye = jnp.where(r128 == c128, 1.0, 0.0).astype(F32)
    logd = logd_ref[...]
    growth = jnp.exp(hdot(incl, logd))
    tail = jnp.exp(hdot(upper, logd))
    for h in range(8):
        lb[h] = jnp.broadcast_to(logd[:, h : h + 1], (128, 128))
        bb[h] = jnp.broadcast_to(beta[:, h : h + 1], (128, 128))
        eg[h] = jnp.broadcast_to(growth[:, h : h + 1], (128, 128))
        et[h] = jnp.broadcast_to(tail[:, h : h + 1], (128, 128))

    def norm(v):
        return v * lax.rsqrt(jnp.sum(v * v, axis=-1, keepdims=True) + 1e-06)

    def across(a, b):
        return lax.dot_general(
            a, b, (((1,), (1,)), ((), ())),
            precision=lax.Precision.HIGHEST, preferred_element_type=F32,
        )

    def head_part(h, base):
        cut = pl.ds(pl.multiple_of(base + h * 128, 128), 128)
        return qkv[:, cut].astype(F32)

    @pl.loop(0, 8 // HU)
    def _(it):
        hs = [it * HU + u for u in range(HU)]
        qs = [norm(head_part(h, 0)) for h in hs]
        ks = [norm(head_part(h, 1024)) for h in hs]
        ratio = [
            jnp.where(r128 >= c128, jnp.exp(hdot(incl, jnp.where(r128 > c128, lb[h], 0.0))), 0.0)
            for h in hs
        ]
        both = [across(jnp.concatenate([k, q], axis=0), k) for k, q in zip(ks, qs)]
        raised = [
            -jnp.where(r128 > c128, bb[h] * ra * bo[:128], 0.0)
            for h, ra, bo in zip(hs, ratio, both)
        ]
        scores = [bo[128:] * ra for bo, ra in zip(both, ratio)]
        running = [eye + r for r in raised]
        for _ in range(6):
            raised = [hdot(r, r) for r in raised]
            running = [w + hdot(w, r) for w, r in zip(running, raised)]
        solved = [
            hdot(
                w,
                jnp.concatenate(
                    [bb[h] * eg[h] * k, bb[h] * head_part(h, 2048)], axis=1
                ),
            )
            for h, w, k in zip(hs, running, ks)
        ]
        moved = [hdot(jnp.transpose(so), et[h] * k) for h, so, k in zip(hs, solved, ks)]
        outs = [hdot(sc, so) for sc, so in zip(scores, solved)]
        for h, q, mo, ou in zip(hs, qs, moved, outs):
            last = eg[h, 127:128, :]
            ab_ref[h, :128, :] = (last * eye - mo[:128]).astype(BF16)
            ab_ref[h, 128:, :] = mo[128:].astype(BF16)
            qp_ref[h] = eg[h] * q - ou[:, :128]
            o0_ref[h] = ou[:, 128:]

            @pl.when(h != i)
            def _():
                a2a_copy(h).start()

    ab_in[i] = ab_ref[i]

    @pl.when(i != 0)
    def _():
        a2a_from(0).wait_recv()

    rows = lax.broadcasted_iota(jnp.int32, (256, 128), 0)
    cols = lax.broadcasted_iota(jnp.int32, (256, 128), 1)
    tp[0] = jnp.where(rows == cols, 1.0, 0.0).astype(F32)
    tp[1] = ab_in[0].astype(F32)

    @pl.loop(1, 8)
    def _(j):
        @pl.when(i != j)
        def _():
            a2a_from(j).wait_recv()

        low = ab_in[j]
        tp[j + 1] = split_dot(tp[j], low[:128]) + jnp.where(rows >= 128, low.astype(F32), 0.0)

    tot_out[...] = tp[8].astype(BF16)

    def tot_copy(g):
        return remote(tot_out, tot_in.at[grp], tot_s.at[g], tot_r.at[grp], (seg, g * 8 + i))

    def tot_from(g):
        return remote(tot_out, tot_in.at[g], tot_s.at[g], tot_r.at[g], (seg, g * 8 + i))

    @pl.loop(grp + 1, 8)
    def _(g):
        tot_copy(g).start()

    for k in range(3, 6):
        w_own(k, 0).start()
        w_own(k, 1).start()

    entering[...] = jnp.zeros((128, 128), F32)

    @pl.loop(0, grp)
    def _(g):
        tot_from(g).wait_recv()
        pair = tot_in[g]
        entering[...] = split_dot(entering[...], pair[:128]) + pair[128:].astype(F32)

    def st_copy(j):
        return remote(s_out.at[j], s_in.at[i], st_s.at[j], st_r.at[i], (seg, grp * 8 + j))

    def st_from(j):
        return remote(s_out.at[j], s_in.at[j], st_s.at[j], st_r.at[j], (seg, grp * 8 + j))

    state = entering[...]
    for j in range(8):
        pre = tp[j]
        s_out[j] = (hdot(state, pre[:128]) + pre[128:]).astype(BF16)

        @pl.when(j != i)
        def _():
            st_copy(j).start()

    s_in[i] = s_out[i]

    w_got(0, 0)
    w_relay(0, 0).start()
    w_got(0, 1)
    w_got(1, 0)
    w_relay(1, 0).start()
    w_got(1, 1)
    w_got(2, 0)
    w_got(2, 1)
    w_relay(0, 1).start()

    for h in range(8):
        @pl.when(h != i)
        def _():
            st_from(h).wait_recv()

    fetches[6].wait()
    for h in range(8):
        qp = qp_ref[h]
        high = qp.astype(BF16)
        low = (qp - high.astype(F32)).astype(BF16)
        dims = (((1,), (1,)), ((), ()))
        o = o0_ref[h] + (
            lax.dot_general(high, s_in[h], dims, preferred_element_type=F32)
            + lax.dot_general(low, s_in[h], dims, preferred_element_type=F32)
        )
        o = o * lax.rsqrt(jnp.mean(o * o, axis=-1, keepdims=True) + 1e-06) * og_ref[...]
        on[:, h * 128 : (h + 1) * 128] = o.astype(BF16)

    hidden = (
        x_ref[...].astype(F32) + jnp.dot(on[...], wo_ref[...], preferred_element_type=F32)
    ).astype(BF16)
    hid[...] = hidden
    hf = hidden.astype(F32)
    hf = hf * lax.rsqrt(jnp.mean(hf * hf, axis=-1, keepdims=True) + 1e-06) * fg_ref[...]
    gath[me - col * 16] = hf.astype(BF16)

    def half(zz, hv):
        return gath.at[lax.rem(zz, 8) * 2 + core, pl.ds(hv * 64, 64)]

    def ag_send(s, hv, way):
        ref = half(z + 8 - s if way == 0 else z + s, hv)
        k = s * 2 + hv
        return remote(ref, ref, ag_s.at[way, k], ag_r.at[way, k], right if way == 0 else left)

    def ag_recv(s, hv, way):
        ref = half(z + 7 - s if way == 0 else z + 1 + s, hv)
        k = s * 2 + hv
        return remote(ref, ref, ag_s.at[way, k], ag_r.at[way, k], right if way == 0 else left)

    def mate_send(dz, hv):
        ref = half(z + dz, hv)
        k = dz * 2 + hv
        return remote(ref, ref, pf_s.at[k], pf_r.at[k], mate)

    def mate_recv(dz, hv):
        ref = gath.at[lax.rem(z + dz, 8) * 2 + 1 - core, pl.ds(hv * 64, 64)]
        k = dz * 2 + hv
        return remote(ref, ref, pf_s.at[k], pf_r.at[k], mate)

    for hv in range(2):
        for way in range(2):
            ag_send(0, hv, way).start()
    for hv in range(2):
        mate_send(0, hv).start()
    w_got(3, 1)
    w_relay(1, 1).start()
    for s in range(1, 4):
        if s == 3:
            w_got(4, 0)
            w_relay(2, 0).start()
            w_got(5, 1)
            w_relay(2, 1).start()
        for hv in range(2):
            for way in range(2):
                ag_recv(s - 1, hv, way).wait_recv()
                if s < 3 or hv == way:
                    ag_send(s, hv, way).start()
                mate_send(8 - s if way == 0 else s, hv).start()
    ag_recv(3, 0, 0).wait_recv()
    mate_send(4, 0).start()
    ag_recv(3, 1, 1).wait_recv()
    mate_send(4, 1).start()
    for dz in range(8):
        for hv in range(2):
            mate_recv(dz, hv).wait_recv()

    for k in range(4):
        xs[pl.ds(k * 128, 128)] = gath[sel_ref[k]]

    def hidden_units(src):
        @pl.loop(0, 2)
        def _(n):
            cut = pl.ds(pl.multiple_of(n * 256, 256), 256)
            gate = jnp.dot(xs[...], wg[src, :, cut], preferred_element_type=F32)
            up = jnp.dot(xs[...], wu[src, :, cut], preferred_element_type=F32)
            act[src, :, cut] = (gate / (1.0 + jnp.exp(-gate)) * up).astype(BF16)

    for c in locals_:
        c.wait()
    hidden_units(col)
    w_got(3, 0)
    hidden_units(xleft)
    hidden_units(xright)
    w_got(5, 0)
    w_got(4, 1)
    for way in range(2):
        for r in range(2):
            w_relay(r, way).wait_recv()
    hidden_units(lax.rem(col + 2, 4))
    for way in range(2):
        w_relay(2, way).wait_recv()

    def mate_part(n):
        return remote(pout.at[n], pin.at[n], px_s.at[n], px_r.at[n], mate)

    def own_part(n, zz):
        b = lax.rem(zz, 8)
        return part[n, tgt_ref[b * 2 + core]].astype(F32) + pin[n, b].astype(F32)

    def ring(n, s, way):
        src, dst, ss, rs, dev = (sr, rr, rr_s, rr_r, right) if way == 0 else (sl, rl, rl_s, rl_r, left)
        lo, cnt = (way * 64, 64) if s == 0 else (0, 128)
        cut = pl.ds(lo, cnt)
        return remote(src.at[n, s, cut], dst.at[n, s, cut], ss.at[n, s], rs.at[n, s], dev)

    def first(n):
        mate_part(n).wait_recv()
        far = own_part(n, z + 4).astype(BF16)
        sr[n, 0, pl.ds(0, 64)] = far[:64]
        sl[n, 0, pl.ds(64, 64)] = far[64:]
        ring(n, 0, 0).start()
        ring(n, 0, 1).start()

    @pl.loop(0, NCH)
    def _(n):
        cut = pl.ds(pl.multiple_of(n * CW, CW), CW)
        total = jnp.dot(act[0], wd[0, :, cut], preferred_element_type=F32)
        for src in range(1, 4):
            total = total + jnp.dot(act[src], wd[src, :, cut], preferred_element_type=F32)
        for k in range(4):
            part[n, k] = total[k * 128 : (k + 1) * 128].astype(BF16)
        part[n, 4] = jnp.zeros((128, CW), BF16)
        for zz in range(8):
            pout[n, zz] = part[n, tgt_ref[zz * 2 + 1 - core]]
        mate_part(n).start()

        @pl.when(n >= 1)
        def _():
            first(n - 1)

    first(NCH - 1)

    for s in range(1, 4):
        @pl.loop(0, NCH)
        def _(n):
            for way in range(2):
                ring(n, s - 1, way).wait_recv()
                here = own_part(n, z + 4 - s if way == 0 else z + 4 + s)
                buf, got = (sr, rr) if way == 0 else (sl, rl)
                if s == 1:
                    lo, other = way * 64, 64 - way * 64
                    buf[n, s, pl.ds(lo, 64)] = (
                        here[lo : lo + 64] + got[n, 0, pl.ds(lo, 64)].astype(F32)
                    ).astype(BF16)
                    buf[n, s, pl.ds(other, 64)] = here[other : other + 64].astype(BF16)
                else:
                    buf[n, s] = (here + got[n, s - 1].astype(F32)).astype(BF16)
                ring(n, s, way).start()

    def y_send(n):
        cut = pl.ds(pl.multiple_of(n * CW, CW), CW)
        return remote(yout.at[n], out_ref.at[:, cut], y_s.at[n], y_r.at[n], yn)

    @pl.loop(0, NCH)
    def _(n):
        for way in range(2):
            ring(n, 3, way).wait_recv()
        cut = pl.ds(pl.multiple_of(n * CW, CW), CW)
        ffn = (own_part(n, z) + rr[n, 3].astype(F32) + rl[n, 3].astype(F32)).astype(BF16)
        yout[n] = (hid[:, cut].astype(F32) + ffn.astype(F32)).astype(BF16)
        y_send(n).start()

    @pl.loop(1, 8)
    def _(k):
        j = lax.rem(i + k, 8)
        a2a_copy(j).wait_send()
        st_copy(j).wait_send()

    @pl.loop(grp + 1, 8)
    def _(g):
        tot_copy(g).wait_send()

    for way in range(2):
        for k in range(6):
            w_own(k, way).wait_send()
        for r in range(3):
            w_relay(r, way).wait_send()
        for s in range(4):
            for hv in range(2):
                if s < 3 or hv == way:
                    ag_send(s, hv, way).wait_send()
    for dz in range(8):
        for hv in range(2):
            mate_send(dz, hv).wait_send()

    @pl.loop(0, NCH)
    def _(n):
        mate_part(n).wait_send()
        for s in range(4):
            for way in range(2):
                ring(n, s, way).wait_send()
        y_send(n).wait()


def run_tick(sel, tgt, x, logd, ng, bw, og, fg, wq, wo, gate, up, down):
    vmem = pl.BlockSpec(memory_space=pltpu.VMEM)
    smem = pl.BlockSpec(memory_space=pltpu.SMEM)
    hbm = pl.BlockSpec(memory_space=pl.ANY)
    V = pltpu.VMEM
    D = pltpu.SemaphoreType.DMA
    return pl.pallas_call(
        tick_kernel,
        out_shape=jax.ShapeDtypeStruct((128, 1024), BF16),
        in_specs=[smem, smem] + [vmem] * 6 + [hbm] * 5,
        out_specs=vmem,
        scratch_shapes=[
            V((1024, 3072), BF16), V((1024, 1024), BF16), V((128, 3072), BF16),
            V((8, 128, 128), F32), V((8, 128, 128), F32), V((8, 128, 128), F32),
            V((8, 128, 128), F32), V((8, 128, 128), F32), V((8, 128, 128), F32),
            V((8, 256, 128), BF16),
            V((8, 256, 128), BF16), V((9, 256, 128), F32), V((256, 128), BF16),
            V((8, 256, 128), BF16), V((8, 128, 128), BF16), V((8, 128, 128), BF16),
            V((128, 1024), BF16), V((128, 1024), BF16), V((16, 128, 1024), BF16),
            V((512, 1024), BF16), V((4, 1024, 512), BF16), V((4, 1024, 512), BF16),
            V((4, 512, 1024), BF16), V((4, 512, 512), BF16), V((NCH, 5, 128, CW), BF16),
            V((NCH, 8, 128, CW), BF16), V((NCH, 8, 128, CW), BF16),
            V((NCH, 4, 128, CW), BF16), V((NCH, 4, 128, CW), BF16),
            V((NCH, 4, 128, CW), BF16), V((NCH, 4, 128, CW), BF16), V((NCH, 128, CW), BF16),
            V((128, 128), F32),
            D((3,)), D((7,)), D((8,)), D((8,)), D((8,)), D((8,)), D((8,)), D((8,)),
            D((2, 9)), D((2, 9)), D((2, 8)), D((2, 8)), D((16,)), D((16,)),
            D((NCH,)), D((NCH,)), D((NCH, 4)), D((NCH, 4)), D((NCH, 4)), D((NCH, 4)),
            D((NCH,)), D((NCH,)),
        ],
        compiler_params=pltpu.CompilerParams(
            collective_id=0, has_side_effects=True, vmem_limit_bytes=60 * 1024 * 1024
        ),
        name="tick",
    )(sel, tgt, x, logd, ng, bw, og, fg, wq, wo, gate, up, down)


def per_device(
    held, log_decay, route_ids, norm_gain, qkv_weight, beta_weight, out_gain, out_weight,
    ffn_gain, gate_weight, up_weight, down_weight,
):
    place = lax.axis_index("seq")
    kinds = lax.dynamic_slice_in_dim(route_ids[0, :, 0], place // 16 * 16, 16)
    index = jnp.arange(16)
    same = (kinds[:, None] == kinds[None, :]) & (index[:, None] // 8 == index[None, :] // 8)
    rank = jnp.sum((same & (index[None, :] < index[:, None])).astype(jnp.int32), axis=1)
    mine = kinds == place % EXPERTS
    tgt = jnp.where(mine, index // 8 * 2 + rank, 4).astype(jnp.int32)
    slots = jnp.arange(4)
    sel = jnp.sum(jnp.where(tgt[None, :] == slots[:, None], index[None, :], 0), axis=1).astype(
        jnp.int32
    )
    out = run_tick(
        sel, tgt, held[0], log_decay[0], norm_gain, beta_weight[0], out_gain, ffn_gain,
        qkv_weight[0], out_weight[0], gate_weight[0, 0], up_weight[0, 0], down_weight[0, 0],
    )
    return out[None]


def solution(mesh):
    placed = (
        P("segment", "seq", None),
        P("segment", "seq", None),
        P("segment", None, None),
        P("segment", None),
        P("segment", None, None),
        P("segment", None, None),
        P("segment", None),
        P("segment", None, None),
        P("segment", None),
        P("segment", "seq", None, None),
        P("segment", "seq", None, None),
        P("segment", "seq", None, None),
    )
    return jax.shard_map(
        per_device, mesh=mesh, in_specs=placed, out_specs=P("segment", "seq", None), check_vma=False
    )
```
